32 devices in a mesh: lon: 8 (over y, x, core), lat: 4 (over z).
Axes of the slice: x: 2, y: 2, z: 4, core: 2. Of those that a mesh axis runs over, the one named last changes fastest.
Arguments:
- tokens: bfloat16 [6, 288, 192, 192], P(None, 'lat', 'lon'), may hold values from -6 to 6
- obs_values: bfloat16 [65536, 256], P(('lon', 'lat')), may hold values from -6 to 6
- obs_dest: int32 [65536], P(('lon', 'lat')), may hold values from 0 to 31, as said below
- obs_cell: int32 [65536], P(('lon', 'lat')), may hold values from 0 to 10367
- obs_count: int32 [32], P(('lon', 'lat')), may hold values from 1365 to 2048, as said below
- w_obs: bfloat16 [256, 192], replicated, may hold values from -0.375 to 0.375
- ln1_gain: float32 [192], replicated, may hold values from 0.1 to 1.9
- w_qkv: bfloat16 [192, 576], replicated, may hold values from -0.4375 to 0.4375
- position_bias: float32 [6, 144, 144], replicated, may hold values from -4 to 400
- w_proj: bfloat16 [192, 192], replicated, may hold values from -0.4375 to 0.4375
- ln2_gain: float32 [192], replicated, may hold values from 0.1 to 1.9
- w_up: bfloat16 [192, 768], replicated, may hold values from -0.4375 to 0.4375
- w_down: bfloat16 [768, 192], replicated, may hold values from -0.21875 to 0.21875
Outputs:
- block_out: bfloat16 [6, 288, 192, 192], P(None, 'lat', 'lon')
The draws below stay inside these ranges and needn't reach their ends.
Inputs may be any that keep to these rules, and one draw needn't show every extreme that they name: `obs_dest`: the tile owning a row, numbered lon index * 4 + lat index; among the live rows of one device no tile is named more than 128 times, and in every draw one tile is named exactly 128 times by the live rows of every device. `obs_cell`: a cell of the owning tile, numbered (level * 72 + row) * 24 + column. The live rows of device s are the first obs_count[s] rows of its block; the others are padding.
All inputs are finite; a program needn't handle non-finite values.
Results may differ from the reference program's by a relative error of at most 0.01.
Values may be sent and summed in bfloat16 or wider, within the bound.
No kernel may reach another device: no remote copies, remote signals or barrier semaphores. Data moves between devices by JAX's collectives and lax.ppermute only.
A program may use at most 128 MiB of HBM per device.

```python
import math
import jax
import jax.numpy as jnp
from jax import lax

D = 192
HEADS = 6
HID = 768
F_OBS = 256
WZ = 2
WLAT = 6
WLON = 12
NZ = 6
LA = 72
LO = 24
OBS_DEV = 2048
WIN = 144
NLAT = 288
NLON = 192
TOK_DEV = 10368
CAP = 128
N_LAT = 4
DEVICES = 32


def routing(key):
    base = jax.random.fold_in(key, 5)
    hot_key, count_key, rest_key = jax.random.split(base, 3)
    hottest = jax.random.randint(hot_key, (), 0, DEVICES)
    counts = jax.random.randint(count_key, (DEVICES,), 2 * OBS_DEV // 3, OBS_DEV + 1)
    pool_ids = jnp.arange(DEVICES * CAP, dtype=jnp.int32) // CAP

    def one_source(source_key, count_live):
        first_key, second_key = jax.random.split(source_key)
        mixed_ids = jax.random.permutation(first_key, pool_ids)
        ranking = jnp.argsort(jnp.where(mixed_ids == hottest, 0, 1), stable=True)
        listed = mixed_ids[ranking][:OBS_DEV]
        position = jnp.arange(OBS_DEV, dtype=jnp.int32)
        random_keys = jax.random.randint(second_key, (OBS_DEV,), 0, 2 ** 30 // OBS_DEV) * OBS_DEV + position
        ordering = jnp.where(position < count_live, random_keys, 2 ** 30 + position)
        placed = jnp.argsort(ordering, stable=True)
        return jnp.zeros((OBS_DEV,), jnp.int32).at[placed].set(listed)
    dest_ids = jax.vmap(one_source)(jax.random.split(rest_key, DEVICES), counts)
    return (dest_ids, counts.astype(jnp.int32))


def draw_obs_dest(key, part):
    return routing(key)[0].reshape(-1)


def draw_obs_count(key, part):
    return routing(key)[1]


def draw_position_bias(key, part):
    base = jax.random.fold_in(key, 11)
    first = jax.random.fold_in(base, 0)
    table_shape = (HEADS, WIN, WIN)
    table = jnp.clip(jax.random.normal(first, table_shape, jnp.float32), -4.0, 4.0)
    return table


def with_ends(array, stream_key, low, top_value):
    spot = [jax.random.randint(jax.random.fold_in(stream_key, axis), (), 0, length) for axis, length in enumerate(array.shape)]
    main_axis = array.shape.index(max(array.shape))
    beside = spot[:main_axis] + [(spot[main_axis] + 1) % array.shape[main_axis]] + spot[main_axis + 1:]
    return array.at[tuple(spot)].set(low).at[tuple(beside)].set(top_value)


def steps_of(own_key, dims, cuts, smallest, high):
    factor_of, own = 1.0, jax.random.fold_in(own_key, 6)
    for dim, shards_of in cuts:
        steps = jnp.exp(jax.random.uniform(jax.random.fold_in(own, dim), (shards_of,), jnp.float32, smallest / len(cuts), high / len(cuts)))
        factor_of = factor_of * jnp.repeat(steps, dims[dim] // shards_of).reshape([-1 if axis == dim else 1 for axis in range(len(dims))])
    return factor_of


def gaussian(key, dims, deviation, limit, shards=(), held_as=jnp.bfloat16):
    level = steps_of(key, dims, shards, -0.22, 0.18) if shards else 1.0
    array = jax.random.normal(key, dims, jnp.float32) * deviation * level
    return jnp.minimum(jnp.maximum(array, -limit), limit).astype(held_as)


def setup_inputs(seed: int = 0) -> dict:
    arg_keys = jax.random.split(jax.random.key(seed), 14)
    tokens = gaussian(arg_keys[0], (NZ, NLAT, NLON, D), 1.0, 6.0, ((1, 4), (2, 8)))
    obs_values = gaussian(arg_keys[1], (DEVICES * OBS_DEV, F_OBS), 1.0, 6.0, ((0, 32),))
    obs_dest = draw_obs_dest(jax.random.fold_in(arg_keys[13], 71), 0)
    obs_cell = with_ends(jax.random.randint(arg_keys[3], (DEVICES * OBS_DEV,), 0, TOK_DEV), jax.random.fold_in(arg_keys[3], 1), 0, TOK_DEV - 1).astype(jnp.int32)
    obs_count = draw_obs_count(jax.random.fold_in(arg_keys[13], 71), 0)
    w_obs = gaussian(arg_keys[5], (F_OBS, D), F_OBS ** -0.5, 0.375)
    ln1_gain = jnp.clip(1.0 + 0.18 * jax.random.normal(arg_keys[6], (D,), jnp.float32), 0.1, 1.9)
    w_qkv = gaussian(arg_keys[7], (D, 3 * D), D ** -0.5, 0.4375)
    position_bias = draw_position_bias(jax.random.fold_in(arg_keys[13], 71), 0)
    w_proj = gaussian(arg_keys[9], (D, D), D ** -0.5, 0.4375)
    ln2_gain = jnp.clip(1.0 + 0.18 * jax.random.normal(arg_keys[10], (D,), jnp.float32), 0.1, 1.9)
    w_up = gaussian(arg_keys[11], (D, HID), D ** -0.5, 0.4375)
    w_down = gaussian(arg_keys[12], (HID, D), HID ** -0.5, 0.21875)
    return dict(tokens=tokens, obs_values=obs_values, obs_dest=obs_dest, obs_cell=obs_cell, obs_count=obs_count, w_obs=w_obs, ln1_gain=ln1_gain, w_qkv=w_qkv, position_bias=position_bias, w_proj=w_proj, ln2_gain=ln2_gain, w_up=w_up, w_down=w_down)


def layer_norm(inputs, gain):
    values32 = inputs.astype(jnp.float32)
    average = lax.optimization_barrier(jnp.mean(values32, axis=-1, keepdims=True))
    centered = values32 - average
    variance = lax.optimization_barrier(jnp.mean(centered * centered, axis=-1, keepdims=True))
    return centered * lax.rsqrt(variance + 1e-05) * gain

def to_windows(grid):
    levels, lat_rows, lon_cols = grid.shape[:3]
    trailing = grid.shape[3:]
    shaped = grid.reshape((levels // WZ, WZ, lat_rows // WLAT, WLAT, lon_cols // WLON, WLON) + trailing)
    axes_order = (2, 0, 4, 1, 3, 5) + tuple(range(6, 6 + len(trailing)))
    return shaped.transpose(axes_order).reshape((lat_rows // WLAT, levels // WZ * (lon_cols // WLON), WZ * WLAT * WLON) + trailing)

def from_windows(windows, levels, lat_rows, lon_cols):
    trailing = windows.shape[3:]
    shaped = windows.reshape((lat_rows // WLAT, levels // WZ, lon_cols // WLON, WZ, WLAT, WLON) + trailing)
    axes_order = (1, 3, 0, 4, 2, 5) + tuple(range(6, 6 + len(trailing)))
    return shaped.transpose(axes_order).reshape((levels, lat_rows, lon_cols) + trailing)

def attend_windows(block, grouped, bias, ln1_gain, w_qkv, w_proj):
    amount, win_size, features = block.shape
    heads = bias.shape[0]
    head_dim = features // heads
    normed = layer_norm(block, ln1_gain).astype(jnp.bfloat16)
    qkv_rows = jnp.dot(normed.reshape(-1, features), w_qkv, preferred_element_type=jnp.float32).astype(jnp.bfloat16)
    qkv_rows = qkv_rows.reshape(amount, win_size, 3, heads, head_dim)
    query = qkv_rows[:, :, 0].astype(jnp.float32)
    key_rows = qkv_rows[:, :, 1].astype(jnp.float32)
    value_rows = qkv_rows[:, :, 2].astype(jnp.float32)
    scores = jnp.einsum('wqhc,wkhc->whqk', query, key_rows)
    scores = scores * (1.0 / math.sqrt(head_dim)) + bias[None]
    allowed = grouped[:, None, :, None] == grouped[:, None, None, :]
    scores = jnp.where(allowed, scores, -1e+30)
    highest = lax.optimization_barrier(jnp.max(scores, axis=-1, keepdims=True))
    weights = jnp.exp(scores - highest)
    prob_bf = (weights / lax.optimization_barrier(jnp.sum(weights, axis=-1, keepdims=True))).astype(jnp.bfloat16)
    context = jnp.einsum('whqk,wkhc->wqhc', prob_bf.astype(jnp.float32), value_rows).astype(jnp.bfloat16)
    mixed_f = jnp.dot(context.reshape(-1, features), w_proj, preferred_element_type=jnp.float32)
    result = (block.reshape(-1, features).astype(jnp.float32) + mixed_f).astype(jnp.bfloat16)
    return result.reshape(amount, win_size, features)

def window_pass(shifted, first_row, total_rows, bias, ln1_gain, w_qkv, w_proj):
    levels, lat_rows, lon_cols = shifted.shape[:3]
    half_z = WZ // 2
    half_lat = WLAT // 2
    rolled = jnp.roll(shifted, -half_z, axis=0)
    anchor = first_row + jnp.arange(lat_rows, dtype=jnp.int32)
    lat_flag = (anchor >= 0) & (anchor < half_lat) | (anchor >= total_rows)
    level_flag = jnp.arange(levels, dtype=jnp.int32) >= levels - half_z
    grouped = 2 * lat_flag.astype(jnp.int32)[None, :, None] + level_flag.astype(jnp.int32)[:, None, None]
    grouped = jnp.broadcast_to(grouped, (levels, lat_rows, lon_cols))
    windows = to_windows(rolled)
    labels = to_windows(grouped[..., None])[..., 0]
    attended = lax.map(lambda operands: attend_windows(operands[0], operands[1], bias, ln1_gain, w_qkv, w_proj), (windows, labels))
    return jnp.roll(from_windows(attended, levels, lat_rows, lon_cols), half_z, axis=0)

def feed_forward(rows_in, ln2_gain, w_up, w_down):
    normed = layer_norm(rows_in, ln2_gain).astype(jnp.bfloat16)
    hidden = jax.nn.gelu(jnp.dot(normed, w_up, preferred_element_type=jnp.float32), approximate=False).astype(jnp.bfloat16)
    return (rows_in.astype(jnp.float32) + jnp.dot(hidden, w_down, preferred_element_type=jnp.float32)).astype(jnp.bfloat16)

def feed_grid(grid, ln2_gain, w_up, w_down):
    blocks = grid.reshape(grid.shape[1] // WLAT, -1, grid.shape[3])
    result = lax.map(lambda rows_in: feed_forward(rows_in, ln2_gain, w_up, w_down), blocks)
    return result.reshape(grid.shape)

def reference(tokens, obs_values, obs_dest, obs_cell, obs_count, w_obs, ln1_gain, w_qkv, position_bias, w_proj, ln2_gain, w_up, w_down):
    embedded = jnp.dot(obs_values, w_obs, preferred_element_type=jnp.float32).astype(jnp.bfloat16)
    row_ids = jnp.arange(DEVICES * OBS_DEV, dtype=jnp.int32)
    is_live = row_ids % OBS_DEV < jnp.repeat(obs_count, OBS_DEV)
    lon_tile = obs_dest // N_LAT
    lat_tile = obs_dest % N_LAT
    level_ids = obs_cell // (LA * LO)
    lat_ids = lat_tile * LA + obs_cell // LO % LA
    lon_ids = lon_tile * LO + obs_cell % LO
    terms = jnp.where(is_live[:, None], embedded.astype(jnp.float32), 0.0)
    obs_field = jnp.zeros((NZ, NLAT, NLON, D), jnp.float32).at[level_ids, lat_ids, lon_ids].add(terms)
    stream = (tokens.astype(jnp.float32) + obs_field).astype(jnp.bfloat16)
    half_lat = WLAT // 2
    half_lon = WLON // 2
    shifted = jnp.roll(stream, (-half_lat, -half_lon), axis=(1, 2))
    attended = window_pass(shifted, half_lat, NLAT, position_bias, ln1_gain, w_qkv, w_proj)
    result = feed_grid(attended, ln2_gain, w_up, w_down)
    return jnp.roll(result, (half_lat, half_lon), axis=(1, 2))
```

```python
import functools
import math

import jax
import jax.numpy as jnp
from jax import lax
from jax.experimental import pallas as pl
from jax.experimental.pallas import tpu as pltpu
from jax.sharding import PartitionSpec as P

WZ = 2
WLAT = 6
WLON = 12

NT = (((1,), (1,)), ((), ()))
TN = (((0,), (0,)), ((), ()))


def layer_norm(x, gain):
    n = x.shape[-1]
    mean = jnp.sum(x, axis=-1, keepdims=True) * (1.0 / n)
    c = x - mean
    var = jnp.sum(c * c, axis=-1, keepdims=True) * (1.0 / n)
    return c * lax.rsqrt(var + 1e-5) * gain


def dot(a, b):
    return jnp.dot(a, b, preferred_element_type=jnp.float32)


def attend_all(xs, tabs, g1, wk, wqv, wproj, heads, lag=1):
    bf, f32 = jnp.bfloat16, jnp.float32
    win, d = xs[0].shape
    hd, tail = d // heads, win - 128
    reps, n = 128 // tail, len(xs)
    nx = [layer_norm(x, g1).astype(bf) for x in xs]
    kk, q, v = [], [], []
    for i in range(n):
        kk.append(dot(nx[i], wk).astype(bf))
        ext = jnp.concatenate([nx[i][:128]] + [nx[i][128:]] * reps, axis=0)
        qv = lax.dot_general(wqv, ext, NT, preferred_element_type=f32)
        q.append((qv[:d] * (math.log2(math.e) / math.sqrt(hd))).astype(bf))
        v.append(qv[d:].astype(bf)[:, :win])
    ones = jnp.ones((16, win), bf)
    zero = jnp.zeros((hd, 128), bf)
    mask = (lax.broadcasted_iota(jnp.int32, (d, 128), 0) // hd) == (lax.broadcasted_iota(jnp.int32, (d, 128), 1) // tail)
    jobs = [(i, p) for i in range(n) for p in range(heads // 2 + 1)]
    s_of, e_of, c_of = {}, {}, {}

    def scores(i, p):
        if p < heads // 2:
            cols = [jnp.concatenate([q[i][hd * h:hd * h + hd, :128] if j == h else zero for j in range(heads)], axis=0)
                    for h in (2 * p, 2 * p + 1)]
            rhs = jnp.concatenate(cols, axis=1)
        else:
            rhs = jnp.where(mask, q[i][:, 128:].astype(f32), 0.0).astype(bf)
        s_of[i, p] = dot(kk[i], rhs) + tabs[i][:, 256 * p:256 * p + rhs.shape[1]]

    def soft(i, p):
        s = s_of.pop((i, p))
        e_of[i, p] = jnp.exp2(s - jnp.max(s, axis=0, keepdims=True)).astype(bf)

    def values(i, p):
        e = e_of.pop((i, p))
        if p < heads // 2:
            o = dot(jnp.concatenate([v[i][2 * hd * p:2 * hd * p + 2 * hd], ones], axis=0), e)
            r = 1.0 / o[2 * hd:2 * hd + 1]
            c_of[i, p] = [(o[:hd, :128] * r[:, :128]).astype(bf), (o[hd:2 * hd, 128:] * r[:, 128:]).astype(bf)]
        else:
            o = dot(jnp.concatenate([v[i], ones], axis=0), e)
            c_of[i, p] = jnp.where(mask, o[:d] * (1.0 / o[d:d + 1]), 0.0).astype(bf)

    ys = []
    def finish(i):
        main = jnp.concatenate([c for p in range(heads // 2) for c in c_of[i, p]], axis=0)
        ctx = jnp.concatenate([main, c_of[i, heads // 2]], axis=1)
        proj = lax.dot_general(ctx, wproj, TN, preferred_element_type=f32)
        fold = proj[128:128 + tail]
        for h in range(1, heads):
            fold = fold + proj[128 + tail * h:128 + tail * h + tail]
        ys.append((xs[i] + jnp.concatenate([proj[:128], fold], axis=0)).astype(bf))

    for t in range(len(jobs) + 2 * lag):
        if t < len(jobs):
            scores(*jobs[t])
        if 0 <= t - lag < len(jobs):
            soft(*jobs[t - lag])
        if 0 <= t - 2 * lag < len(jobs):
            values(*jobs[t - 2 * lag])
            if jobs[t - 2 * lag][1] == heads // 2:
                finish(jobs[t - 2 * lag][0])
    return ys


def ffn_all(ys, g2, wup, wdown):
    bf = jnp.bfloat16
    n2 = [layer_norm(y.astype(jnp.float32), g2).astype(bf) for y in ys]
    outs = []
    for i in range(len(ys)):
        u = dot(n2[i], wup)
        h = (0.5 * u * (1.0 + lax.erf(u * (1.0 / math.sqrt(2.0))))).astype(bf)
        outs.append((ys[i].astype(jnp.float32) + dot(h, wdown)).astype(bf))
    return outs


def passed_along(block, axis, distance):
    devices = range(lax.axis_size(axis))
    route = [((i - distance) % len(devices), i) for i in devices]
    return lax.ppermute(block, axis, route)


def to_windows(grid):
    levels, lat_rows, lon_cols = grid.shape[:3]
    trailing = grid.shape[3:]
    shaped = grid.reshape(
        (levels // WZ, WZ, lat_rows // WLAT, WLAT, lon_cols // WLON, WLON) + trailing
    )
    axes_order = (2, 0, 4, 1, 3, 5) + tuple(range(6, 6 + len(trailing)))
    return shaped.transpose(axes_order).reshape(
        (lat_rows // WLAT, levels // WZ * (lon_cols // WLON), WZ * WLAT * WLON) + trailing
    )


def from_windows(windows, levels, lat_rows, lon_cols):
    trailing = windows.shape[3:]
    shaped = windows.reshape(
        (lat_rows // WLAT, levels // WZ, lon_cols // WLON, WZ, WLAT, WLON) + trailing
    )
    axes_order = (1, 3, 0, 4, 2, 5) + tuple(range(6, 6 + len(trailing)))
    return shaped.transpose(axes_order).reshape((levels, lat_rows, lon_cols) + trailing)


def window_kernel(heads, lag, pick, x_ref, tab_ref, g1, wk, wqv, wproj, g2, wup, wdown, o_ref):
    xs = [x_ref[0, w].astype(jnp.float32) for w in range(len(pick))]
    tabs = [tab_ref.at[0, p] for p in pick]
    ys = attend_all(xs, tabs, g1[...], wk[...], wqv[...], wproj[...], heads, lag)
    for w, out in enumerate(ffn_all(ys, g2[...], wup[...], wdown[...])):
        o_ref[0, w] = out


def window_blocks(x, tabs, pick, weights, heads, lag=1):
    rows, amount, win, d = x.shape
    last = rows - 1
    full = lambda a: pl.BlockSpec(a.shape, lambda i: (0,) * a.ndim)
    block = pl.BlockSpec((1, amount, win, d), lambda i: (i, 0, 0, 0))
    return pl.pallas_call(
        functools.partial(window_kernel, heads, lag, pick),
        grid=(rows,),
        out_shape=jax.ShapeDtypeStruct(x.shape, x.dtype),
        in_specs=[
            block,
            pl.BlockSpec((1,) + tabs.shape[1:], lambda i: (jnp.where(i == last, 1, 0), 0, 0, 0)),
        ]
        + [full(a) for a in weights],
        out_specs=block,
    )(x, tabs, *weights)


def bias_tables(bias, closed):
    heads, win = bias.shape[:2]
    base = (bias * math.log2(math.e)).transpose(2, 0, 1)
    position = jnp.arange(win, dtype=jnp.int32)
    level = position // (WLAT * WLON)
    half = (position // WLON) % WLAT // (WLAT // 2)
    apart = lambda g: jnp.where(g[:, None] != g[None, :], -1e30, 0.0).astype(jnp.float32)
    by_level, by_row = apart(level), jnp.where(closed, apart(half), 0.0)

    def lanes(t):
        t = jnp.broadcast_to(t, base.shape)
        main = t[:, :, :128].reshape(win, heads * 128)
        tail = t[:, :, 128:].reshape(win, heads * (win - 128))
        return jnp.concatenate([main, tail, jnp.zeros((win, 128 - tail.shape[1]), t.dtype)], axis=1)

    cuts = [jnp.zeros_like(by_level), by_level, by_row, by_level + by_row]
    tables = jnp.stack([lanes(base + c[:, None, :]) for c in cuts])
    return tables.reshape((2, 2) + tables.shape[1:])


def on_device(
    tokens,
    obs_values,
    obs_dest,
    obs_cell,
    obs_count,
    w_obs,
    ln1_gain,
    w_qkv,
    position_bias,
    w_proj,
    ln2_gain,
    w_up,
    w_down,
):
    levels, lat_rows, lon_cols, features = tokens.shape
    lon_count = lax.axis_size("lon")
    lat_count = lax.axis_size("lat")
    devices = lon_count * lat_count
    row_count = obs_values.shape[0]
    capacity = 2 * row_count // devices
    position = jnp.arange(row_count, dtype=jnp.int32)
    is_live = position < obs_count[0]
    matches = (
        (obs_dest[:, None] == jnp.arange(devices, dtype=jnp.int32)[None, :]) & is_live[:, None]
    ).astype(jnp.int32)
    earlier = jnp.cumsum(matches, axis=0) - matches
    slot_ids = jnp.sum(earlier * matches, axis=1)
    targets = jnp.where(is_live, obs_dest * capacity + slot_ids, devices * capacity)
    cell_ids = jnp.zeros((devices * capacity,), jnp.int32).at[targets].set(obs_cell, mode="drop")
    payload = jnp.dot(obs_values, w_obs, preferred_element_type=jnp.float32).astype(jnp.bfloat16)
    buffer = (
        jnp.zeros((devices * capacity, payload.shape[1]), jnp.bfloat16)
        .at[targets]
        .set(payload, mode="drop")
    )
    received, got_cells = (
        lax.all_to_all(buffer, ("lon", "lat"), split_axis=0, concat_axis=0, tiled=True),
        lax.all_to_all(cell_ids, ("lon", "lat"), split_axis=0, concat_axis=0, tiled=True),
    )
    obs_field = (
        jnp.zeros((levels * lat_rows * lon_cols, features), jnp.float32)
        .at[got_cells]
        .add(received.astype(jnp.float32))
    )
    stream = (tokens.astype(jnp.float32) + obs_field.reshape(tokens.shape)).astype(jnp.bfloat16)
    half_lat = WLAT // 2
    half_lon = WLON // 2
    lat_index = lax.axis_index("lat")
    arrived = passed_along(stream[:, :, :half_lon], "lon", -1)
    widened = jnp.concatenate([stream[:, :, half_lon:], arrived], axis=2)
    arrived = passed_along(widened[:, :half_lat], "lat", -1)
    shifted = jnp.concatenate([widened[:, half_lat:], arrived], axis=1)
    heads = position_bias.shape[0]
    windows = to_windows(jnp.roll(shifted, -(WZ // 2), axis=0))
    tables = bias_tables(position_bias, lat_index == lat_count - 1)
    pairs, across = levels // WZ, lon_cols // WLON
    pick = [1 if p == pairs - 1 else 0 for p in range(pairs) for _ in range(across)]
    w_key = w_qkv[:, features : 2 * features]
    w_rest = jnp.concatenate([w_qkv[:, :features], w_qkv[:, 2 * features :]], axis=1).T
    weights = (ln1_gain[None], w_key, w_rest, w_proj, ln2_gain[None], w_up, w_down)
    done = window_blocks(windows, tables, pick, weights, heads)
    result = jnp.roll(from_windows(done, levels, lat_rows, lon_cols), WZ // 2, axis=0)
    arrived = passed_along(result[:, lat_rows - half_lat :], "lat", 1)
    widened = jnp.concatenate([arrived, result[:, : lat_rows - half_lat]], axis=1)
    arrived = passed_along(widened[:, :, lon_cols - half_lon :], "lon", 1)
    return jnp.concatenate([arrived, widened[:, :, : lon_cols - half_lon]], axis=2)


def solution(mesh):
    in_specs = (
        P(None, "lat", "lon", None),
        P(("lon", "lat"), None),
        P(("lon", "lat")),
        P(("lon", "lat")),
        P(("lon", "lat")),
        P(),
        P(),
        P(),
        P(),
        P(),
        P(),
        P(),
        P(),
    )
    out_specs = P(None, "lat", "lon", None)
    return jax.shard_map(
        on_device, mesh=mesh, in_specs=in_specs, out_specs=out_specs, check_vma=False
    )
```

```python
import functools
import math

import jax
import jax.numpy as jnp
import numpy as np
from jax import lax
from jax.experimental import pallas as pl
from jax.experimental.pallas import tpu as pltpu
from jax.sharding import PartitionSpec as P

WZ = 2
WLAT = 6
WLON = 12

NT = (((1,), (1,)), ((), ()))
TN = (((0,), (0,)), ((), ()))


def layer_norm(x, gain):
    n = x.shape[-1]
    mean = jnp.sum(x, axis=-1, keepdims=True) * (1.0 / n)
    c = x - mean
    var = jnp.sum(c * c, axis=-1, keepdims=True) * (1.0 / n)
    return c * lax.rsqrt(var + 1e-5) * gain


def dot(a, b):
    return jnp.dot(a, b, preferred_element_type=jnp.float32)


def attend_all(xs, tabs, g1, wk, wqv, wproj, heads, lag=1):
    bf, f32 = jnp.bfloat16, jnp.float32
    win, d = xs[0].shape
    hd, tail = d // heads, win - 128
    reps, n = 128 // tail, len(xs)
    nx = [layer_norm(x, g1).astype(bf) for x in xs]
    kk, q, v = [], [], []
    for i in range(n):
        kk.append(dot(nx[i], wk).astype(bf))
        ext = jnp.concatenate([nx[i][:128]] + [nx[i][128:]] * reps, axis=0)
        qv = lax.dot_general(wqv, ext, NT, preferred_element_type=f32)
        q.append((qv[:d] * (math.log2(math.e) / math.sqrt(hd))).astype(bf))
        v.append(qv[d:].astype(bf)[:, :win])
    ones = jnp.ones((16, win), bf)
    zero = jnp.zeros((hd, 128), bf)
    mask = (lax.broadcasted_iota(jnp.int32, (d, 128), 0) // hd) == (lax.broadcasted_iota(jnp.int32, (d, 128), 1) // tail)
    jobs = [(i, p) for i in range(n) for p in range(heads // 2 + 1)]
    s_of, e_of, c_of = {}, {}, {}

    def scores(i, p):
        if p < heads // 2:
            cols = [jnp.concatenate([q[i][hd * h:hd * h + hd, :128] if j == h else zero for j in range(heads)], axis=0)
                    for h in (2 * p, 2 * p + 1)]
            rhs = jnp.concatenate(cols, axis=1)
        else:
            rhs = jnp.where(mask, q[i][:, 128:].astype(f32), 0.0).astype(bf)
        s_of[i, p] = dot(kk[i], rhs) + tabs[i][:, 256 * p:256 * p + rhs.shape[1]]

    def soft(i, p):
        s = s_of.pop((i, p))
        e_of[i, p] = jnp.exp2(s - jnp.max(s, axis=0, keepdims=True)).astype(bf)

    def values(i, p):
        e = e_of.pop((i, p))
        if p < heads // 2:
            o = dot(jnp.concatenate([v[i][2 * hd * p:2 * hd * p + 2 * hd], ones], axis=0), e)
            r = 1.0 / o[2 * hd:2 * hd + 1]
            c_of[i, p] = [(o[:hd, :128] * r[:, :128]).astype(bf), (o[hd:2 * hd, 128:] * r[:, 128:]).astype(bf)]
        else:
            o = dot(jnp.concatenate([v[i], ones], axis=0), e)
            c_of[i, p] = jnp.where(mask, o[:d] * (1.0 / o[d:d + 1]), 0.0).astype(bf)

    ys = []
    def finish(i):
        main = jnp.concatenate([c for p in range(heads // 2) for c in c_of[i, p]], axis=0)
        ctx = jnp.concatenate([main, c_of[i, heads // 2]], axis=1)
        proj = lax.dot_general(ctx, wproj, TN, preferred_element_type=f32)
        fold = proj[128:128 + tail]
        for h in range(1, heads):
            fold = fold + proj[128 + tail * h:128 + tail * h + tail]
        ys.append((xs[i] + jnp.concatenate([proj[:128], fold], axis=0)).astype(bf))

    for t in range(len(jobs) + 2 * lag):
        if t < len(jobs):
            scores(*jobs[t])
        if 0 <= t - lag < len(jobs):
            soft(*jobs[t - lag])
        if 0 <= t - 2 * lag < len(jobs):
            values(*jobs[t - 2 * lag])
            if jobs[t - 2 * lag][1] == heads // 2:
                finish(jobs[t - 2 * lag][0])
    return ys


def ffn_all(ys, g2, wup, wdown):
    bf = jnp.bfloat16
    n2 = [layer_norm(y.astype(jnp.float32), g2).astype(bf) for y in ys]
    outs = []
    for i in range(len(ys)):
        u = dot(n2[i], wup)
        h = (0.5 * u * (1.0 + lax.erf(u * (1.0 / math.sqrt(2.0))))).astype(bf)
        outs.append((ys[i].astype(jnp.float32) + dot(h, wdown)).astype(bf))
    return outs


def window_kernel(heads, amount, *refs):
    tab_ref, last_ref, g1, wk, wqv, wproj, g2, wup, wdown = refs[amount : amount + 9]
    outs = refs[-amount:]
    rows, pairs = refs[0].shape[:2]
    xs, tabs = [], []
    for r in range(rows):
        for p in range(pairs):
            parts = [x[r, p].astype(jnp.float32) for x in refs[:amount]]
            xs.append(parts[0] if amount == 1 else jnp.concatenate(parts, axis=0))
            cut = 1 if p == pairs - 1 else 0
            tabs.append(last_ref.at[0, cut] if r == rows - 1 else tab_ref.at[0, cut])
    ys = attend_all(xs, tabs, g1[...], wk[...], wqv[...], wproj[...], heads)
    for w, y in enumerate(ffn_all(ys, g2[...], wup[...], wdown[...])):
        first = 0
        for o in outs:
            size = o.shape[2]
            piece = y if amount == 1 else y.astype(jnp.float32)[first : first + size].astype(y.dtype)
            o[w // pairs, w % pairs] = piece
            first += size


def window_blocks(arrays, tables, weights, heads, steps, in_step, out_step, total, wraps, kept=None):
    pairs = arrays[0].shape[1]
    full = lambda a: pl.BlockSpec(a.shape, lambda i: (0,) * a.ndim)
    rows = lambda a, first: pl.BlockSpec((2,) + a.shape[1:], lambda i: (first + i, 0, 0, 0))
    table = lambda pick: pl.BlockSpec((1,) + tables.shape[1:], pick)
    last = lambda i: (jnp.where(i == steps - 1, 1, 0) if wraps else 0, 0, 0, 0)
    shapes = [jax.ShapeDtypeStruct((total,) + a.shape[1:], a.dtype) for a in arrays]
    specs = [rows(a, in_step) for a in arrays] + [table(lambda i: (0, 0, 0, 0)), table(last)]
    specs = specs + [full(a) for a in weights]
    operands = list(arrays) + [tables, tables] + list(weights)
    aliases = {}
    if kept is not None:
        specs.append(pl.BlockSpec(memory_space=pl.ANY))
        aliases = {len(operands): 0}
        operands.append(kept)
    tokens = steps * 2 * pairs * sum(a.shape[2] for a in arrays)
    return pl.pallas_call(
        functools.partial(window_kernel, heads, len(arrays)),
        grid=(steps,),
        out_shape=shapes,
        in_specs=specs,
        out_specs=[rows(a, out_step) for a in arrays],
        input_output_aliases=aliases,
        cost_estimate=pl.CostEstimate(flops=tokens * 2000000, bytes_accessed=tokens * 800, transcendentals=tokens * 1500),
    )(*operands)


def bias_tables(bias, closed, order):
    heads, win = bias.shape[:2]
    base = (bias[:, order][:, :, order] * math.log2(math.e)).transpose(2, 0, 1)
    level = order // (WLAT * WLON)
    half = (order // WLON) % WLAT // (WLAT // 2)
    apart = lambda g: np.where(g[:, None] != g[None, :], -1e30, 0.0).astype(np.float32)
    by_level, by_row = apart(level), jnp.where(closed, apart(half), 0.0)

    def lanes(t):
        main = t[:, :, :128].reshape(win, heads * 128)
        tail = t[:, :, 128:].reshape(win, heads * (win - 128))
        return jnp.concatenate([main, tail, jnp.zeros((win, 128 - tail.shape[1]), t.dtype)], axis=1)

    plain = lanes(base)
    spread = lambda c: lanes(jnp.broadcast_to(c[:, None, :], base.shape))
    cuts = [jnp.zeros_like(plain), spread(by_level), spread(by_row), spread(by_level + by_row)]
    tables = jnp.stack([plain + c for c in cuts])
    return tables.reshape((2, 2) + tables.shape[1:])


def token_order(first_col, cols):
    half, level, row, col = np.meshgrid(
        np.arange(2), np.arange(WZ), np.arange(WLAT // 2), np.arange(cols), indexing="ij"
    )
    return ((level * WLAT + half * (WLAT // 2) + row) * WLON + first_col + col).reshape(-1)


def dispatch_kernel(cap, total, count_ref, dest_ref, payload_ref, out_ref, target_ref):
    bf, f32, i32 = jnp.bfloat16, jnp.float32, jnp.int32
    n = dest_ref.shape[1]
    group = out_ref.shape[0]

    @pl.when(pl.program_id(0) == 0)
    def _():
        dest = dest_ref[...]
        lane = lax.broadcasted_iota(i32, (1, n), 1)
        owner = lax.broadcasted_iota(i32, (total, n), 0)
        hit = (dest == owner) & (lane < count_ref[0])
        hits = jnp.where(hit, 1.0, 0.0)
        upper = lax.broadcasted_iota(i32, (128, 128), 0) < lax.broadcasted_iota(i32, (128, 128), 1)
        upper = jnp.where(upper, 1.0, 0.0).astype(bf)
        base = (lax.broadcasted_iota(i32, (total, 1), 0) * cap).astype(f32)
        for b in range(n // 128):
            block = hits[:, 128 * b : 128 * b + 128]
            slot = dot(block.astype(bf), upper) + base
            found = jnp.sum(block * slot, axis=0, keepdims=True)
            live = jnp.sum(block, axis=0, keepdims=True)
            target_ref[:, 128 * b : 128 * b + 128] = jnp.where(live > 0.5, found, -1.0).astype(i32)
            base = base + jnp.sum(block, axis=1, keepdims=True)

    rows = group * cap
    slot = pl.program_id(0) * rows + lax.broadcasted_iota(i32, (rows, 1), 0)
    chosen = jnp.where(target_ref[...] == slot, 1.0, 0.0).astype(bf)
    moved = dot(chosen, payload_ref[...])
    pick = lax.broadcasted_iota(i32, (8, 128), 0) + 64 == lax.broadcasted_iota(i32, (8, 128), 1)
    pick = jnp.where(pick, 1.0, 0.0).astype(bf)
    low = lax.broadcasted_iota(i32, (cap // 2, 128), 1) < 64
    for g in range(group):
        part = moved[g * cap : g * cap + cap]
        tail = part[:, 128:]
        packed = jnp.where(low, tail[: cap // 2], pltpu.roll(tail[cap // 2 :], 64, 1))
        cells = lax.dot_general(pick, tail.astype(bf), NT, preferred_element_type=f32)
        if cap < 128:
            cells = jnp.concatenate([cells, jnp.zeros((8, 128 - cap), f32)], axis=1)
        out_ref[g] = jnp.concatenate([part[:, :128], packed, cells], axis=0).astype(bf)


def dispatch(count, dest, payload, devices, cap):
    group = 512 // cap
    rows = cap + cap // 2 + 8
    n = dest.shape[0]
    return pl.pallas_call(
        functools.partial(dispatch_kernel, cap, devices),
        grid=(devices // group,),
        out_shape=jax.ShapeDtypeStruct((devices, rows, 128), jnp.bfloat16),
        in_specs=[
            pl.BlockSpec(memory_space=pltpu.SMEM),
            pl.BlockSpec((1, n), lambda i: (0, 0)),
            pl.BlockSpec(payload.shape, lambda i: (0, 0)),
        ],
        out_specs=pl.BlockSpec((group, rows, 128), lambda i: (i, 0, 0)),
        scratch_shapes=[pltpu.VMEM((1, n), jnp.int32)],
    )(count, dest[None], payload)


def collect_kernel(cap, levels, lat_rows, codes, got, tok, mid, right, left, field, held, win):
    bf, f32, i32 = jnp.bfloat16, jnp.float32, jnp.int32
    lines, features = tok.shape[0], tok.shape[2]
    rest = features - 128

    def fill(q, _):
        t = tok[q].astype(f32)
        field[0, q] = t[:, :128]
        field[1, q, :, :rest] = t[:, 128:]
        field[1, q, :, rest:] = jnp.zeros((t.shape[0], 128 - rest), f32)
        return 0

    lax.fori_loop(0, lines, fill, 0, unroll=4)
    rowi = lax.broadcasted_iota(i32, (cap, cap), 0)
    coli = lax.broadcasted_iota(i32, (cap, cap), 1)
    ones = jnp.ones((cap, cap), bf)
    near = (rowi // 8 == coli // 8) & (coli <= rowi)

    def source(s, _):
        digits = got[s, cap + cap // 2 :, :].astype(f32)
        same = near
        for k in range(2):
            along = jnp.broadcast_to(digits[k : k + 1, :cap], (cap, cap))
            down = dot(jnp.where(rowi == coli, along, 0.0).astype(bf), ones)
            same = same & (along == down)
        same = jnp.where(same, 1.0, 0.0).astype(bf)
        held[0] = dot(same, got[s, :cap, :])
        t = got[s, cap : cap + cap // 2, :].astype(f32)
        held[1] = dot(same, jnp.concatenate([t, pltpu.roll(t, 64, 1)], axis=0).astype(bf))

        for b in range(cap // 8):
            places = [codes[s * cap + 8 * b + j] for j in range(8)]
            spots = [(c >> 5, pl.ds(c & 31, 1)) for c in places]
            sums = [[field[k, q, o, :] + held[k, 8 * b + j : 8 * b + j + 1, :] for k in range(2)]
                    for j, (q, o) in enumerate(spots)]
            for (q, o), pair in zip(spots, sums):
                for k in range(2):
                    field[k, q, o, :] = pair[k]
        return 0

    lax.fori_loop(0, got.shape[0], source, 0)
    half_lat, pairs = WLAT // 2, levels // WZ
    wins = lat_rows // WLAT

    def cut(l, _):
        for p in range(pairs):
            for out, first, cols in ((mid, WLON // 2, WLON), (right, WLON + WLON // 2, WLON // 2), (left, 0, WLON // 2)):
                at = 0
                for half in range(2):
                    for lev in range(WZ):
                        z = (WZ * p + WZ // 2 + lev) % levels
                        for row in range(half_lat):
                            a = half_lat + WLAT * l + half_lat * half + row
                            a = jnp.where(a >= lat_rows, a - lat_rows, a)
                            for k in range(2):
                                win[k, at : at + cols, :] = field[k, z * lat_rows + a, first : first + cols, :]
                            at += cols
                out[l, p, :, :128] = win[0, :at, :].astype(bf)
                out[l, p, :, 128:] = win[1, :at, :rest].astype(bf)
        return 0

    lax.fori_loop(0, wins, cut, 0)


def collect(codes, got, tokens, cap):
    levels, lat_rows, lon_cols, features = tokens.shape
    wins, pairs = lat_rows // WLAT, levels // WZ
    shape = lambda t: jax.ShapeDtypeStruct((wins, pairs, t, features), jnp.bfloat16)
    full, part = WZ * WLAT * WLON, WZ * WLAT * WLON // 2
    lines = levels * lat_rows
    vmem = pl.BlockSpec(memory_space=pltpu.VMEM)
    return pl.pallas_call(
        functools.partial(collect_kernel, cap, levels, lat_rows),
        out_shape=[shape(full), shape(part), shape(part)],
        in_specs=[pl.BlockSpec(memory_space=pltpu.SMEM), vmem, vmem],
        out_specs=[vmem] * 3,
        scratch_shapes=[
            pltpu.VMEM((2, lines, lon_cols, 128), jnp.float32),
            pltpu.VMEM((2, cap, 128), jnp.float32),
            pltpu.VMEM((2, full, 128), jnp.float32),
        ],
    )(codes, got, tokens.reshape(lines, lon_cols, features))


def join_kernel(levels, mid, right, left, out, win):
    f32 = jnp.float32
    half_lat, pairs = WLAT // 2, levels // WZ
    rest = out.shape[3] - 128
    half = (pl.program_id(0) + 2 * pl.num_programs(0) - 1) % 2
    for p in range(pairs):
        base = 0
        for part, cols in ((left, WLON // 2), (mid, WLON), (right, WLON // 2)):
            x = part[0, p].astype(f32)
            if part is mid:
                size = x.shape[0]
            else:
                size = x.shape[0] // 2
                x = jnp.where(half == 0, x[:size], x[size:])
            at = 0
            for lev in range(WZ):
                z = (WZ * p + WZ // 2 + lev) % levels
                for row in range(half_lat):
                    piece = x[at : at + cols]
                    win[0, z * half_lat + row, base : base + cols, :] = piece[:, :128]
                    win[1, z * half_lat + row, base : base + cols, :rest] = piece[:, 128:]
                    at += cols
            base += cols
    for z in range(levels):
        for row in range(half_lat):
            out[z, row, :, :128] = win[0, z * half_lat + row].astype(out.dtype)
            out[z, row, :, 128:] = win[1, z * half_lat + row, :, :rest].astype(out.dtype)


def join(mid, right, left, levels, lat_rows, lon_cols):
    half_lat = WLAT // 2
    units = lat_rows // half_lat
    features = mid.shape[-1]
    unit = lambda u: (u + units - 1) % units
    whole = lambda a: pl.BlockSpec((1,) + a.shape[1:], lambda u: (unit(u) // 2, 0, 0, 0))
    halved = pl.BlockSpec((1, mid.shape[1], mid.shape[2] // 2, features), lambda u: (unit(u) // 2, 0, unit(u) % 2, 0))
    return pl.pallas_call(
        functools.partial(join_kernel, levels),
        grid=(units,),
        out_shape=jax.ShapeDtypeStruct((levels, lat_rows, lon_cols, features), mid.dtype),
        in_specs=[halved, whole(right), whole(left)],
        out_specs=pl.BlockSpec((levels, half_lat, lon_cols, features), lambda u: (0, u, 0, 0)),
        scratch_shapes=[pltpu.VMEM((2, levels * half_lat, lon_cols, 128), jnp.float32)],
    )(mid, right, left)


def sent(block, lon, lat):
    lons, lats = lax.axis_size("lon"), lax.axis_size("lat")
    at = lambda i, j: (i % lons) * lats + j % lats
    route = [(at(i, j), at(i + lon, j + lat)) for i in range(lons) for j in range(lats)]
    return lax.ppermute(block, ("lon", "lat"), route)


def on_device(
    tokens,
    obs_values,
    obs_dest,
    obs_cell,
    obs_count,
    w_obs,
    ln1_gain,
    w_qkv,
    position_bias,
    w_proj,
    ln2_gain,
    w_up,
    w_down,
):
    levels, lat_rows, lon_cols, features = tokens.shape
    lat_count = lax.axis_size("lat")
    devices = lax.axis_size("lon") * lat_count
    row_count = obs_values.shape[0]
    cap = 2 * row_count // devices
    bf = jnp.bfloat16
    payload = jnp.dot(obs_values, w_obs, preferred_element_type=jnp.float32).astype(bf)
    digits = jnp.stack([obs_cell // 128, obs_cell % 128], axis=1).astype(bf)
    payload = jnp.concatenate([payload, digits, jnp.zeros((row_count, 62), bf)], axis=1)
    buffer = dispatch(obs_count, obs_dest, payload, devices, cap)
    got = lax.all_to_all(buffer, ("lon", "lat"), split_axis=0, concat_axis=0, tiled=True)
    body = cap + cap // 2
    high, low = (got[:, body + k, :cap].astype(jnp.int32) for k in range(2))
    cells = (high * 128 + low).reshape(-1)
    codes = (cells // lon_cols) * 32 + cells % lon_cols

    heads = position_bias.shape[0]
    closed = lax.axis_index("lat") == lat_count - 1
    half = WLON // 2
    inner = bias_tables(position_bias, closed, token_order(0, WLON))
    outer = np.concatenate([token_order(0, half), token_order(half, half)])
    outer = bias_tables(position_bias, closed, outer)
    w_key = w_qkv[:, features : 2 * features]
    w_rest = jnp.concatenate([w_qkv[:, :features], w_qkv[:, 2 * features :]], axis=1).T
    weights = (ln1_gain[None], w_key, w_rest, w_proj, ln2_gain[None], w_up, w_down)

    mid, right, left = collect(codes, got, tokens, cap)
    wins = mid.shape[0]
    part = right.shape[2] // 2
    arrived = sent(left, -1, 0)
    below_mid = sent(mid[-1:, :, 2 * part :], 0, -1)
    below_right = sent(right[-1:, :, part:], 0, -1)
    below_left = sent(left[-1:, :, part:], -1, -1)

    first = wins // 2 // 2
    tail = wins // 2 - 1
    done = window_blocks([mid], inner, weights, heads, first, 0, 0, wins, False)[0]
    right_in = lax.dynamic_update_slice(right, below_right, (wins - 1, 0, part, 0))
    left_in = lax.dynamic_update_slice(arrived, below_left, (wins - 1, 0, part, 0))
    right_out, left_out = window_blocks([right_in, left_in], outer, weights, heads, wins // 2, 0, 0, wins, True)
    home_left = sent(left_out, 1, 0)
    home_right = sent(right_out[-1:, :, part:], 0, 1)
    home_corner = sent(left_out[-1:, :, part:], 1, 1)
    edge = jnp.concatenate([mid[-1:, :, : 2 * part], below_mid], axis=2)
    edge = jnp.concatenate([mid[-2:-1], edge], axis=0)
    done = window_blocks([edge], inner, weights, heads, 1, 0, tail, wins, True, done)[0]
    home_mid = sent(done[-1:, :, 2 * part :], 0, 1)
    done = window_blocks([mid], inner, weights, heads, tail - first, first, first, wins, False, done)[0]

    done = lax.dynamic_update_slice(done, home_mid, (wins - 1, 0, 2 * part, 0))
    right_out = lax.dynamic_update_slice(right_out, home_right, (wins - 1, 0, part, 0))
    home_left = lax.dynamic_update_slice(home_left, home_corner, (wins - 1, 0, part, 0))
    return join(done, right_out, home_left, levels, lat_rows, lon_cols)


def solution(mesh):
    in_specs = (
        P(None, "lat", "lon", None),
        P(("lon", "lat"), None),
        P(("lon", "lat")),
        P(("lon", "lat")),
        P(("lon", "lat")),
        P(),
        P(),
        P(),
        P(),
        P(),
        P(),
        P(),
        P(),
    )
    out_specs = P(None, "lat", "lon", None)
    return jax.shard_map(
        on_device, mesh=mesh, in_specs=in_specs, out_specs=out_specs, check_vma=False
    )
```

```python
import functools
import math

import jax
import jax.numpy as jnp
import numpy as np
from jax import lax
from jax.experimental import pallas as pl
from jax.experimental.pallas import tpu as pltpu
from jax.sharding import PartitionSpec as P

WZ = 2
WLAT = 6
WLON = 12

NT = (((1,), (1,)), ((), ()))
TN = (((0,), (0,)), ((), ()))


def layer_norm(x, gain):
    n = x.shape[-1]
    mean = jnp.sum(x, axis=-1, keepdims=True) * (1.0 / n)
    c = x - mean
    var = jnp.sum(c * c, axis=-1, keepdims=True) * (1.0 / n)
    return c * lax.rsqrt(var + 1e-5) * gain


def dot(a, b):
    return jnp.dot(a, b, preferred_element_type=jnp.float32)


def attend_all(xs, tab, masks, g1, wk, wqv, wproj, heads, lag=1):
    bf, f32 = jnp.bfloat16, jnp.float32
    win, d = xs[0].shape
    hd, tail = d // heads, win - 128
    reps, n = 128 // tail, len(xs)
    nx = [layer_norm(x, g1).astype(bf) for x in xs]
    kk, q, v = [], [], []
    for i in range(n):
        kk.append(dot(nx[i], wk).astype(bf))
        ext = jnp.concatenate([nx[i][:128]] + [nx[i][128:]] * reps, axis=0)
        qv = lax.dot_general(wqv, ext, NT, preferred_element_type=f32)
        q.append((qv[:d] * (math.log2(math.e) / math.sqrt(hd))).astype(bf))
        v.append(qv[d:].astype(bf)[:, :win])
    ones = jnp.ones((16, win), bf)
    zero = jnp.zeros((hd, 128), bf)
    mask = (lax.broadcasted_iota(jnp.int32, (d, 128), 0) // hd) == (lax.broadcasted_iota(jnp.int32, (d, 128), 1) // tail)
    jobs = [(i, p) for i in range(n) for p in range(heads // 2 + 1)]
    s_of, e_of, c_of = {}, {}, {}

    def scores(i, p):
        if p < heads // 2:
            cols = [jnp.concatenate([q[i][hd * h:hd * h + hd, :128] if j == h else zero for j in range(heads)], axis=0)
                    for h in (2 * p, 2 * p + 1)]
            rhs = jnp.concatenate(cols, axis=1)
        else:
            rhs = jnp.where(mask, q[i][:, 128:].astype(f32), 0.0).astype(bf)
        s = dot(kk[i], rhs) + tab[:, 256 * p:256 * p + rhs.shape[1]]
        for m in masks[i]:
            cut = jnp.concatenate([m[:, :128]] * 2, axis=1) if p < heads // 2 else m[:, 128:]
            s = s + cut
        s_of[i, p] = s

    def soft(i, p):
        s = s_of.pop((i, p))
        e_of[i, p] = jnp.exp2(s - jnp.max(s, axis=0, keepdims=True)).astype(bf)

    def values(i, p):
        e = e_of.pop((i, p))
        if p < heads // 2:
            o = dot(jnp.concatenate([v[i][2 * hd * p:2 * hd * p + 2 * hd], ones], axis=0), e)
            r = 1.0 / o[2 * hd:2 * hd + 1]
            c_of[i, p] = [(o[:hd, :128] * r[:, :128]).astype(bf), (o[hd:2 * hd, 128:] * r[:, 128:]).astype(bf)]
        else:
            o = dot(jnp.concatenate([v[i], ones], axis=0), e)
            c_of[i, p] = jnp.where(mask, o[:d] * (1.0 / o[d:d + 1]), 0.0).astype(bf)

    ys = []
    def finish(i):
        main = jnp.concatenate([c for p in range(heads // 2) for c in c_of[i, p]], axis=0)
        ctx = jnp.concatenate([main, c_of[i, heads // 2]], axis=1)
        proj = lax.dot_general(ctx, wproj, TN, preferred_element_type=f32)
        fold = proj[128:128 + tail]
        for h in range(1, heads):
            fold = fold + proj[128 + tail * h:128 + tail * h + tail]
        ys.append((xs[i] + jnp.concatenate([proj[:128], fold], axis=0)).astype(bf))

    for t in range(len(jobs) + 2 * lag):
        if t < len(jobs):
            scores(*jobs[t])
        if 0 <= t - lag < len(jobs):
            soft(*jobs[t - lag])
        if 0 <= t - 2 * lag < len(jobs):
            values(*jobs[t - 2 * lag])
            if jobs[t - 2 * lag][1] == heads // 2:
                finish(jobs[t - 2 * lag][0])
    return ys


def ffn_all(ys, g2, wup, wdown):
    bf = jnp.bfloat16
    n2 = [layer_norm(y.astype(jnp.float32), g2).astype(bf) for y in ys]
    outs = []
    for i in range(len(ys)):
        u = dot(n2[i], wup)
        h = (0.5 * u * (1.0 + lax.erf(u * (1.0 / math.sqrt(2.0))))).astype(bf)
        outs.append((ys[i].astype(jnp.float32) + dot(h, wdown)).astype(bf))
    return outs


def window_kernel(heads, amount, wraps, *refs):
    tab_ref, cut_ref, last_ref, g1, wk, wqv, wproj, g2, wup, wdown = refs[amount : amount + 10]
    outs = refs[-amount:]
    rows, pairs = refs[0].shape[:2]
    xs, masks = [], []
    for r in range(rows):
        for p in range(pairs):
            parts = [x[r, p].astype(jnp.float32) for x in refs[:amount]]
            xs.append(parts[0] if amount == 1 else jnp.concatenate(parts, axis=0))
            masks.append([])
            if p == pairs - 1:
                masks[-1].append(cut_ref.at[0])
            if wraps and r == rows - 1:
                masks[-1].append(last_ref.at[0])
    ys = attend_all(xs, tab_ref, masks, g1[...], wk[...], wqv[...], wproj[...], heads)
    for w, y in enumerate(ffn_all(ys, g2[...], wup[...], wdown[...])):
        first = 0
        for o in outs:
            size = o.shape[2]
            piece = y if amount == 1 else y.astype(jnp.float32)[first : first + size].astype(y.dtype)
            o[w // pairs, w % pairs] = piece
            first += size


def window_blocks(arrays, tables, weights, heads, steps, in_step, out_step, total, wraps, kept=None):
    pairs = arrays[0].shape[1]
    full = lambda a: pl.BlockSpec(a.shape, lambda i: (0,) * a.ndim)
    rows = lambda a, first: pl.BlockSpec((2,) + a.shape[1:], lambda i: (first + i, 0, 0, 0))
    table, masks = tables
    mask = lambda pick: pl.BlockSpec((1,) + masks.shape[1:], lambda i: (pick(i), 0, 0))
    last = lambda i: jnp.where(i == steps - 1, 1, 2)
    shapes = [jax.ShapeDtypeStruct((total,) + a.shape[1:], a.dtype) for a in arrays]
    specs = [rows(a, in_step) for a in arrays] + [full(table), mask(lambda i: 0), mask(last)]
    specs = specs + [full(a) for a in weights]
    operands = list(arrays) + [table, masks, masks] + list(weights)
    aliases = {}
    if kept is not None:
        specs.append(pl.BlockSpec(memory_space=pl.ANY))
        aliases = {len(operands): 0}
        operands.append(kept)
    tokens = steps * 2 * pairs * sum(a.shape[2] for a in arrays)
    return pl.pallas_call(
        functools.partial(window_kernel, heads, len(arrays), wraps),
        grid=(steps,),
        out_shape=shapes,
        in_specs=specs,
        out_specs=[rows(a, out_step) for a in arrays],
        input_output_aliases=aliases,
        cost_estimate=pl.CostEstimate(flops=tokens * 2000000, bytes_accessed=tokens * 800, transcendentals=tokens * 1500),
    )(*operands)


def table_kernel(orders, bias_ref, *refs):
    heads, win = bias_ref.shape[:2]
    f32 = jnp.float32
    exact = functools.partial(lax.dot_general, precision=lax.Precision.HIGHEST, preferred_element_type=f32)
    for order, out in zip(refs[:orders], refs[orders:]):
        chosen = order[...]
        tails = []
        for h in range(heads):
            turned = exact(chosen, bias_ref[h] * math.log2(math.e), NT)
            t = exact(turned, chosen, NT)
            out[:, 128 * h : 128 * h + 128] = t[:, :128]
            tails.append(t[:, 128:])
        width = heads * (win - 128)
        out[:, 128 * heads :] = jnp.concatenate(tails + [jnp.zeros((win, 128 - width), f32)], axis=1)


def bias_tables(bias, orders):
    heads, win = bias.shape[:2]
    chosen = [np.eye(win, dtype=np.float32)[o] for o in orders]
    shape = jax.ShapeDtypeStruct((win, heads * 128 + 128), jnp.float32)
    return pl.pallas_call(
        functools.partial(table_kernel, len(orders)),
        out_shape=[shape] * len(orders),
        cost_estimate=pl.CostEstimate(flops=10**10, bytes_accessed=10**7, transcendentals=0),
    )(bias, *chosen)


def group_masks(closed, order):
    win = len(order)
    tail = win - 128
    level = order // (WLAT * WLON)
    half = (order // WLON) % WLAT // (WLAT // 2)
    lanes = np.concatenate([np.arange(128), 128 + np.arange(128) % tail])
    apart = lambda g: np.where(g[:, None] != g[None, lanes], -1e30, 0.0).astype(np.float32)
    return jnp.stack([apart(level), jnp.where(closed, apart(half), 0.0), np.zeros((win, 256), np.float32)])


def token_order(first_col, cols):
    half, level, row, col = np.meshgrid(
        np.arange(2), np.arange(WZ), np.arange(WLAT // 2), np.arange(cols), indexing="ij"
    )
    return ((level * WLAT + half * (WLAT // 2) + row) * WLON + first_col + col).reshape(-1)


def dispatch_kernel(cap, total, count_ref, dest_ref, payload_ref, out_ref, target_ref):
    bf, f32, i32 = jnp.bfloat16, jnp.float32, jnp.int32
    n = dest_ref.shape[1]
    group = out_ref.shape[0]

    @pl.when(pl.program_id(0) == 0)
    def _():
        dest = dest_ref[...]
        lane = lax.broadcasted_iota(i32, (1, n), 1)
        owner = lax.broadcasted_iota(i32, (total, n), 0)
        hit = (dest == owner) & (lane < count_ref[0])
        hits = jnp.where(hit, 1.0, 0.0)
        upper = lax.broadcasted_iota(i32, (128, 128), 0) < lax.broadcasted_iota(i32, (128, 128), 1)
        upper = jnp.where(upper, 1.0, 0.0).astype(bf)
        base = (lax.broadcasted_iota(i32, (total, 1), 0) * cap).astype(f32)
        for b in range(n // 128):
            block = hits[:, 128 * b : 128 * b + 128]
            slot = dot(block.astype(bf), upper) + base
            found = jnp.sum(block * slot, axis=0, keepdims=True)
            live = jnp.sum(block, axis=0, keepdims=True)
            target_ref[:, 128 * b : 128 * b + 128] = jnp.where(live > 0.5, found, -1.0).astype(i32)
            base = base + jnp.sum(block, axis=1, keepdims=True)

    rows = group * cap
    slot = pl.program_id(0) * rows + lax.broadcasted_iota(i32, (rows, 1), 0)
    chosen = jnp.where(target_ref[...] == slot, 1.0, 0.0).astype(bf)
    moved = dot(chosen, payload_ref[...])
    pick = lax.broadcasted_iota(i32, (8, 128), 0) + 64 == lax.broadcasted_iota(i32, (8, 128), 1)
    pick = jnp.where(pick, 1.0, 0.0).astype(bf)
    low = lax.broadcasted_iota(i32, (cap // 2, 128), 1) < 64
    for g in range(group):
        part = moved[g * cap : g * cap + cap]
        tail = part[:, 128:]
        packed = jnp.where(low, tail[: cap // 2], pltpu.roll(tail[cap // 2 :], 64, 1))
        cells = lax.dot_general(pick, tail.astype(bf), NT, preferred_element_type=f32)
        if cap < 128:
            cells = jnp.concatenate([cells, jnp.zeros((8, 128 - cap), f32)], axis=1)
        out_ref[g] = jnp.concatenate([part[:, :128], packed, cells], axis=0).astype(bf)


def dispatch(count, dest, payload, devices, cap):
    group = 512 // cap
    rows = cap + cap // 2 + 8
    n = dest.shape[0]
    return pl.pallas_call(
        functools.partial(dispatch_kernel, cap, devices),
        grid=(devices // group,),
        out_shape=jax.ShapeDtypeStruct((devices, rows, 128), jnp.bfloat16),
        in_specs=[
            pl.BlockSpec(memory_space=pltpu.SMEM),
            pl.BlockSpec((1, n), lambda i: (0, 0)),
            pl.BlockSpec(payload.shape, lambda i: (0, 0)),
        ],
        out_specs=pl.BlockSpec((group, rows, 128), lambda i: (i, 0, 0)),
        scratch_shapes=[pltpu.VMEM((1, n), jnp.int32)],
    )(count, dest[None], payload)


def gather_rows(cap, codes, got, tok, field, held):
    bf, f32, i32 = jnp.bfloat16, jnp.float32, jnp.int32
    lines, features = tok.shape[0], tok.shape[2]
    rest = features - 128
    def fill(q, _):
        t = tok[q].astype(f32)
        field[0, q] = t[:, :128]
        field[1, q, :, :rest] = t[:, 128:]
        field[1, q, :, rest:] = jnp.zeros((t.shape[0], 128 - rest), f32)
        return 0

    lax.fori_loop(0, lines, fill, 0, unroll=4)
    rowi = lax.broadcasted_iota(i32, (cap, cap), 0)
    coli = lax.broadcasted_iota(i32, (cap, cap), 1)
    ones = jnp.ones((cap, cap), bf)
    near = (rowi // 8 == coli // 8) & (coli <= rowi)

    def source(s, _):
        digits = got[s, cap + cap // 2 :, :].astype(f32)
        same = near
        for k in range(2):
            along = jnp.broadcast_to(digits[k : k + 1, :cap], (cap, cap))
            down = dot(jnp.where(rowi == coli, along, 0.0).astype(bf), ones)
            same = same & (along == down)
        same = jnp.where(same, 1.0, 0.0).astype(bf)
        held[0] = dot(same, got[s, :cap, :])
        t = got[s, cap : cap + cap // 2, :].astype(f32)
        held[1] = dot(same, jnp.concatenate([t, pltpu.roll(t, 64, 1)], axis=0).astype(bf))

        for b in range(cap // 8):
            places = [codes[s * cap + 8 * b + j] for j in range(8)]
            spots = [(c >> 5, pl.ds(c & 31, 1)) for c in places]
            sums = [[field[k, q, o, :] + held[k, 8 * b + j : 8 * b + j + 1, :] for k in range(2)]
                    for j, (q, o) in enumerate(spots)]
            for (q, o), pair in zip(spots, sums):
                for k in range(2):
                    field[k, q, o, :] = pair[k]
        return 0

    lax.fori_loop(0, got.shape[0], source, 0)


def collect_kernel(cap, levels, lat_rows, codes, got, tok, mid, right, left, field, held, win):
    @pl.when(pl.program_id(0) == 0)
    def _():
        gather_rows(cap, codes, got, tok, field, held)

    half_lat, pairs = WLAT // 2, levels // WZ
    rest = tok.shape[2] - 128
    l = pl.program_id(0)
    for p in range(pairs):
        for n, (out, first, cols) in enumerate(((mid, WLON // 2, WLON), (right, WLON + WLON // 2, WLON // 2), (left, 0, WLON // 2))):
            at = 0
            for half in range(2):
                for lev in range(WZ):
                    z = (WZ * p + WZ // 2 + lev) % levels
                    for row in range(half_lat):
                        a = half_lat + WLAT * l + half_lat * half + row
                        a = jnp.where(a >= lat_rows, a - lat_rows, a)
                        for k in range(2):
                            win[3 * p + n, k, at : at + cols, :] = field[k, z * lat_rows + a, first : first + cols, :]
                        at += cols
            out[0, p, :, :128] = win[3 * p + n, 0, :at, :].astype(out.dtype)
            out[0, p, :, 128:] = win[3 * p + n, 1, :at, :rest].astype(out.dtype)


def collect(codes, got, tokens, cap):
    levels, lat_rows, lon_cols, features = tokens.shape
    wins, pairs = lat_rows // WLAT, levels // WZ
    shape = lambda t: jax.ShapeDtypeStruct((wins, pairs, t, features), jnp.bfloat16)
    full, part = WZ * WLAT * WLON, WZ * WLAT * WLON // 2
    lines = levels * lat_rows
    vmem = pl.BlockSpec(memory_space=pltpu.VMEM)
    return pl.pallas_call(
        functools.partial(collect_kernel, cap, levels, lat_rows),
        out_shape=[shape(full), shape(part), shape(part)],
        grid=(wins,),
        in_specs=[pl.BlockSpec(memory_space=pltpu.SMEM), vmem, vmem],
        out_specs=[pl.BlockSpec((1, pairs, t, features), lambda l: (l, 0, 0, 0)) for t in (full, part, part)],
        scratch_shapes=[
            pltpu.VMEM((2, lines, lon_cols, 128), jnp.float32),
            pltpu.VMEM((2, cap, 128), jnp.float32),
            pltpu.VMEM((3 * pairs, 2, full, 128), jnp.float32),
        ],
    )(codes, got, tokens.reshape(lines, lon_cols, features))


def join_kernel(levels, mid, right, left, out, win, held):
    f32 = jnp.float32
    half_lat, pairs = WLAT // 2, levels // WZ
    rest = out.shape[3] - 128
    half = (pl.program_id(0) + 2 * pl.num_programs(0) - 1) % 2
    for p in range(pairs):
        base = 0
        for n, (part, cols) in enumerate(((left, WLON // 2), (mid, WLON), (right, WLON // 2))):
            x = part[0, p].astype(f32)
            size = x.shape[0]
            slot = 3 * p + n
            held[slot, 0, :size, :] = x[:, :128]
            held[slot, 1, :size, :rest] = x[:, 128:]
            start = 0 if part is mid else half * (size // 2)
            at = 0
            for lev in range(WZ):
                z = (WZ * p + WZ // 2 + lev) % levels
                for row in range(half_lat):
                    for k in range(2):
                        piece = held[slot, k, pl.ds(start + at, cols), :]
                        win[k, z * half_lat + row, base : base + cols, :] = piece
                    at += cols
            base += cols
    for z in range(levels):
        for row in range(half_lat):
            out[z, row, :, :128] = win[0, z * half_lat + row].astype(out.dtype)
            out[z, row, :, 128:] = win[1, z * half_lat + row, :, :rest].astype(out.dtype)


def join(mid, right, left, levels, lat_rows, lon_cols):
    half_lat = WLAT // 2
    units = lat_rows // half_lat
    features = mid.shape[-1]
    unit = lambda u: (u + units - 1) % units
    whole = lambda a: pl.BlockSpec((1,) + a.shape[1:], lambda u: (unit(u) // 2, 0, 0, 0))
    halved = pl.BlockSpec((1, mid.shape[1], mid.shape[2] // 2, features), lambda u: (unit(u) // 2, 0, unit(u) % 2, 0))
    return pl.pallas_call(
        functools.partial(join_kernel, levels),
        grid=(units,),
        out_shape=jax.ShapeDtypeStruct((levels, lat_rows, lon_cols, features), mid.dtype),
        in_specs=[halved, whole(right), whole(left)],
        out_specs=pl.BlockSpec((levels, half_lat, lon_cols, features), lambda u: (0, u, 0, 0)),
        scratch_shapes=[
            pltpu.VMEM((2, levels * half_lat, lon_cols, 128), jnp.float32),
            pltpu.VMEM((3 * (levels // WZ), 2, right.shape[2], 128), jnp.float32),
        ],
    )(mid, right, left)


def sent(block, lon, lat):
    lons, lats = lax.axis_size("lon"), lax.axis_size("lat")
    at = lambda i, j: (i % lons) * lats + j % lats
    route = [(at(i, j), at(i + lon, j + lat)) for i in range(lons) for j in range(lats)]
    return lax.ppermute(block, ("lon", "lat"), route)


def cell_codes(got, cap, lon_cols):
    body = cap + cap // 2
    high, low = (got[:, body + k, :cap].astype(jnp.int32) for k in range(2))
    cells = (high * 128 + low).reshape(-1)
    return (cells // lon_cols) * 32 + cells % lon_cols


def on_device(
    tokens,
    obs_values,
    obs_dest,
    obs_cell,
    obs_count,
    w_obs,
    ln1_gain,
    w_qkv,
    position_bias,
    w_proj,
    ln2_gain,
    w_up,
    w_down,
):
    levels, lat_rows, lon_cols, features = tokens.shape
    lat_count = lax.axis_size("lat")
    devices = lax.axis_size("lon") * lat_count
    row_count = obs_values.shape[0]
    cap = 2 * row_count // devices
    bf = jnp.bfloat16
    payload = jnp.dot(obs_values, w_obs, preferred_element_type=jnp.float32).astype(bf)
    digits = jnp.stack([obs_cell // 128, obs_cell % 128], axis=1).astype(bf)
    payload = jnp.concatenate([payload, digits, jnp.zeros((row_count, 62), bf)], axis=1)
    buffer = dispatch(obs_count, obs_dest, payload, devices, cap)
    got = lax.all_to_all(buffer, ("lon", "lat"), split_axis=0, concat_axis=0, tiled=True)
    heads = position_bias.shape[0]
    closed = lax.axis_index("lat") == lat_count - 1
    half = WLON // 2
    orders = [token_order(0, WLON), np.concatenate([token_order(0, half), token_order(half, half)])]
    inner, outer = [(t, group_masks(closed, o)) for t, o in zip(bias_tables(position_bias, orders), orders)]
    w_key = w_qkv[:, features : 2 * features]
    w_rest = jnp.concatenate([w_qkv[:, :features], w_qkv[:, 2 * features :]], axis=1).T
    weights = (ln1_gain[None], w_key, w_rest, w_proj, ln2_gain[None], w_up, w_down)

    got, inner, outer, weights = lax.optimization_barrier((got, inner, outer, weights))
    codes = cell_codes(got, cap, lon_cols)
    mid, right, left = collect(codes, got, tokens, cap)
    wins = mid.shape[0]
    part = right.shape[2] // 2
    arrived = sent(left, -1, 0)
    below_mid = sent(mid[-1:, :, 2 * part :], 0, -1)
    below_right = sent(right[-1:, :, part:], 0, -1)
    below_left = sent(left[-1:, :, part:], -1, -1)

    first = wins // 2 // 2
    tail = wins // 2 - 1
    done = window_blocks([mid], inner, weights, heads, first, 0, 0, wins, False)[0]
    right_in = lax.dynamic_update_slice(right, below_right, (wins - 1, 0, part, 0))
    left_in = lax.dynamic_update_slice(arrived, below_left, (wins - 1, 0, part, 0))
    right_in, left_in, below_mid, done = lax.optimization_barrier((right_in, left_in, below_mid, done))
    right_out, left_out = window_blocks([right_in, left_in], outer, weights, heads, wins // 2, 0, 0, wins, True)
    right_out, left_out, done = lax.optimization_barrier((right_out, left_out, done))
    home_left = sent(left_out, 1, 0)
    home_right = sent(right_out[-1:, :, part:], 0, 1)
    home_corner = sent(left_out[-1:, :, part:], 1, 1)
    edge = jnp.concatenate([mid[-1:, :, : 2 * part], below_mid], axis=2)
    edge = jnp.concatenate([mid[-2:-1], edge], axis=0)
    done = window_blocks([edge], inner, weights, heads, 1, 0, tail, wins, True, done)[0]
    home_mid = sent(done[-1:, :, 2 * part :], 0, 1)
    done = window_blocks([mid], inner, weights, heads, tail - first, first, first, wins, False, done)[0]

    done = lax.dynamic_update_slice(done, home_mid, (wins - 1, 0, 2 * part, 0))
    right_out = lax.dynamic_update_slice(right_out, home_right, (wins - 1, 0, part, 0))
    home_left = lax.dynamic_update_slice(home_left, home_corner, (wins - 1, 0, part, 0))
    return join(done, right_out, home_left, levels, lat_rows, lon_cols)


def solution(mesh):
    in_specs = (
        P(None, "lat", "lon", None),
        P(("lon", "lat"), None),
        P(("lon", "lat")),
        P(("lon", "lat")),
        P(("lon", "lat")),
        P(),
        P(),
        P(),
        P(),
        P(),
        P(),
        P(),
        P(),
    )
    out_specs = P(None, "lat", "lon", None)
    return jax.shard_map(
        on_device, mesh=mesh, in_specs=in_specs, out_specs=out_specs, check_vma=False
    )
```
